256 devices in a mesh: row: 8 (over z), col: 16 (over x, y), ka: 2 (over core).
Axes of the slice: x: 4, y: 4, z: 8, core: 2. Of those that a mesh axis runs over, the one named last changes fastest.
Arguments:
- iterate: float32 [2560, 13824], P('row', ('col', 'ka')), may hold values from -0.03125 to 0.03125
Outputs:
- update: bfloat16 [2560, 13824], P('row', ('col', 'ka'))
The draws below stay inside these ranges and needn't reach their ends.
All inputs are finite; a program needn't handle non-finite values.
Results may differ from the reference program's by a relative error of at most 0.02.
Values may be sent and summed in bfloat16 or wider, within the bound.
No kernel may reach another device: no remote copies, remote signals or barrier semaphores. Data moves between devices by JAX's collectives and lax.ppermute only.
A program may use at most 64 MiB of HBM per device.

```python
import math
import jax
import jax.numpy as jnp

M = 2560
K = 13824
ITERS = 2


def levels(key, shape, shards, smallest, high):
    factor_of = 1.0
    for dim, blocks in shards:
        steps = jax.random.uniform(jax.random.fold_in(jax.random.fold_in(key, 6), dim), (blocks,), jnp.float32, smallest / len(shards), high / len(shards))
        factor_of = factor_of * jnp.repeat(jnp.exp(steps), shape[dim] // blocks).reshape((-1,) + (1,) * (len(shape) - 1 - dim))
    return factor_of


def bell_draw(stream_key, shape, scale, reach, shards=(), kind=jnp.bfloat16):
    gain = levels(stream_key, shape, shards, -0.22, 0.18) if shards else 1.0
    array = jax.random.normal(stream_key, shape, jnp.float32) * scale * gain
    return jnp.minimum(jnp.maximum(array, -reach), reach).astype(kind)


def setup_inputs(seed: int = 0) -> dict:
    splits = jax.random.split(jax.random.key(seed), 2)
    return {
        "iterate": bell_draw(splits[0], (M, K), (3 * K) ** -0.5, 0.03125, ((0, 8), (1, 32)), jnp.float32),
    }


LINEAR_COEF = 3.4445
CUBIC_COEF = -4.775
QUINTIC_COEF = 2.0315

def reference(iterate):
    current = iterate
    result = None
    for step in range(ITERS):
        rounded = current.astype(jnp.bfloat16)
        gram = jnp.dot(rounded, rounded.T, preferred_element_type=jnp.float32).astype(jnp.bfloat16)
        first = jnp.dot(gram, rounded, preferred_element_type=jnp.float32).astype(jnp.bfloat16)
        second = jnp.dot(gram, first, preferred_element_type=jnp.float32)
        current = LINEAR_COEF * current + CUBIC_COEF * first.astype(jnp.float32) + QUINTIC_COEF * second
    result = (math.sqrt(K) * current).astype(jnp.bfloat16)
    return result
```

```python
import math

import jax
import jax.numpy as jnp
from jax import lax
from jax.sharding import PartitionSpec as P

K = 13824

LINEAR_COEF = 3.4445
CUBIC_COEF = -4.775
QUINTIC_COEF = 2.0315


BF = jnp.bfloat16
F32 = jnp.float32


def shift(array, axis, step):
    n = lax.axis_size(axis)
    return lax.ppermute(array, axis, [((i + step) % n, i) for i in range(n)])


def ring_gather(array, axis):
    n = lax.axis_size(axis)
    blocks = [None] * n
    blocks[0] = array
    for step in range(1, n // 2 + 1):
        blocks[step] = shift(blocks[step - 1], axis, 1)
        if n - step > step:
            blocks[n - step] = shift(blocks[(n - step + 1) % n], axis, -1)
    return jnp.concatenate(blocks, axis=0)


def swap(array):
    return lax.ppermute(array, "ka", [(0, 1), (1, 0)])


def halves_in_order(mine, theirs):
    first = lax.axis_index("ka") == 0
    return jnp.concatenate([jnp.where(first, mine, theirs), jnp.where(first, theirs, mine)], axis=0)


def from_everyone(array, axis):
    n = lax.axis_size(axis)
    return lax.all_to_all(jnp.broadcast_to(array[None], (n, *array.shape)), axis, 0, 0, tiled=True)


def panel_of(block):
    gathered = from_everyone(block, "col")
    mine = gathered.reshape(-1, block.shape[1])
    return halves_in_order(mine, swap(mine))


def slab_of(block):
    gathered = from_everyone(block.T, "row")
    return gathered.reshape(-1, block.shape[0])


def contract(a, b):
    return lax.dot_general(a, b, (((0,), (0,)), ((), ())), preferred_element_type=F32)


def body(iterate):
    rows = iterate.shape[0]
    z = lax.axis_index("row")
    ka = lax.axis_index("ka")
    xb = iterate.astype(BF)
    around = ring_gather(xb, "row")
    total = around.shape[0]
    half = total // 2

    def from_here(array):
        return lax.dynamic_slice_in_dim(jnp.concatenate([array, array], axis=0), z * rows, total, 0)

    part = lax.dot_general(around, xb, (((1,), (1,)), ((), ())), preferred_element_type=F32).astype(BF)
    part = lax.dynamic_slice_in_dim(jnp.concatenate([part, part], axis=0), total - z * rows, total, 0)
    theirs = lax.dynamic_slice_in_dim(part, (1 - ka) * half, half, 0)
    mine = lax.dynamic_slice_in_dim(part, ka * half, half, 0)
    summed = (mine.astype(F32) + swap(theirs).astype(F32)).astype(BF)
    cols = lax.axis_size("col")
    pieces = lax.all_to_all(summed.reshape(cols, half // cols, rows), "col", 0, 0, tiled=True)
    gram = jnp.sum(pieces.astype(F32), axis=0)

    gram_b = gram.astype(BF)
    gram_panel = panel_of(gram_b)
    gram_slab = slab_of(gram_b)
    square = contract(gram_slab, gram_panel)
    poly = (CUBIC_COEF * gram_b.astype(F32) + QUINTIC_COEF * square).astype(BF)
    poly_panel = panel_of(poly)
    once = LINEAR_COEF * iterate + contract(from_here(poly_panel), around)
    once_b = once.astype(BF)
    once_around = ring_gather(once_b, "row")
    cubic = LINEAR_COEF * gram_b.astype(F32) + contract(gram_slab, poly_panel)
    gram1 = LINEAR_COEF * cubic + contract(slab_of(cubic.astype(BF)), poly_panel)
    gram1_b = gram1.astype(BF)
    gram1_panel = panel_of(gram1_b)
    square1 = contract(slab_of(gram1_b), gram1_panel)
    poly1 = (CUBIC_COEF * gram1_b.astype(F32) + QUINTIC_COEF * square1).astype(BF)
    poly1_panel = panel_of(poly1)
    twice = LINEAR_COEF * once + contract(from_here(poly1_panel), once_around)
    return (math.sqrt(K) * twice).astype(BF)


def solution(mesh):
    in_specs = (P("row", ("col", "ka")),)
    out_specs = P("row", ("col", "ka"))
    return jax.shard_map(body, mesh=mesh, in_specs=in_specs, out_specs=out_specs, check_vma=False)
```

```python
import math

import jax
import jax.numpy as jnp
from jax import lax
from jax.sharding import PartitionSpec as P

K = 13824

LINEAR_COEF = 3.4445
CUBIC_COEF = -4.775
QUINTIC_COEF = 2.0315


BF = jnp.bfloat16
F32 = jnp.float32


def shift(array, axis, step):
    n = lax.axis_size(axis)
    return lax.ppermute(array, axis, [((i + step) % n, i) for i in range(n)])


def tie(*arrays):
    return lax.optimization_barrier(arrays)


def put(out, block, place, dim):
    return lax.dynamic_update_slice_in_dim(out, block, place * block.shape[dim], dim)


def in_order(blocks, axis):
    n = lax.axis_size(axis)
    here = lax.axis_index(axis)
    out = jnp.zeros((n * blocks[0].shape[0], *blocks[0].shape[1:]), blocks[0].dtype)
    for step, block in enumerate(blocks):
        out = put(out, block, lax.rem(here + step, n), 0)
    return out


def ring_gather(array, axis):
    n = lax.axis_size(axis)
    here = lax.axis_index(axis)

    def step(s, carry):
        out, up, down = carry
        later = shift(up, axis, 1), shift(down, axis, -1)
        out = put(out, up, lax.rem(here + s, n), 0)
        out = put(out, down, lax.rem(here + n - s, n), 0)
        return (out, *later)

    out = jnp.zeros((n * array.shape[0], *array.shape[1:]), array.dtype)
    out, up, _ = lax.fori_loop(0, n // 2, step, (out, array, array))
    return put(out, up, lax.rem(here + n // 2, n), 0)


class Ring:
    def __init__(self, array, axis):
        self.axis, self.n = axis, lax.axis_size(axis)
        self.blocks = [None] * self.n
        self.blocks[0] = array
        self.step = 0

    def hop(self):
        self.step += 1
        s, n = self.step, self.n
        self.blocks[s] = shift(self.blocks[s - 1], self.axis, 1)
        if n - s > s:
            self.blocks[n - s] = shift(self.blocks[(n - s + 1) % n], self.axis, -1)

    def tie(self, array):
        s, n = self.step, self.n
        at = [s] if n - s <= s else [s, n - s]
        out = tie(*(self.blocks[i] for i in at), array)
        for i, block in zip(at, out):
            self.blocks[i] = block
        return out[-1]


def swap(array):
    return lax.ppermute(array, "ka", [(0, 1), (1, 0)])


def from_everyone(array, axis):
    n = lax.axis_size(axis)
    return lax.all_to_all(jnp.broadcast_to(array[None], (n, *array.shape)), axis, 0, 0, tiled=True)


def panel_of(block):
    mine = from_everyone(block, "col")
    theirs = swap(mine)
    first = lax.axis_index("ka") == 0
    both = jnp.concatenate([jnp.where(first, mine, theirs), jnp.where(first, theirs, mine)], axis=0)
    return both.reshape(-1, block.shape[1])


def slab_of(block):
    gathered = from_everyone(block, "row")
    return jnp.moveaxis(gathered, 0, 1).reshape(block.shape[0], -1)


def slab_by_permutes(block):
    n = lax.axis_size("row")
    gathered = in_order([block[None]] + [shift(block[None], "row", s) for s in range(1, n)], "row")
    return jnp.moveaxis(gathered, 0, 1).reshape(block.shape[0], -1)


def product(slab, panel):
    return jnp.dot(slab, panel, preferred_element_type=F32)


def apply(panel, whole):
    return lax.dot_general(panel, whole, (((0,), (0,)), ((), ())), preferred_element_type=F32)


def body(iterate):
    rows = iterate.shape[0]
    ka = lax.axis_index("ka")
    cols = lax.axis_size("col")
    xb = iterate.astype(BF)
    whole = ring_gather(xb, "row")

    part = lax.dot_general(whole, xb, (((1,), (1,)), ((), ())), preferred_element_type=F32).astype(BF)
    part = part.reshape(2, cols, -1, rows)
    theirs = lax.dynamic_index_in_dim(part, 1 - ka, 0, keepdims=False)
    mine = lax.dynamic_index_in_dim(part, ka, 0, keepdims=False)
    summed = (mine.astype(F32) + swap(theirs).astype(F32)).astype(BF)
    pieces = lax.all_to_all(summed, "col", 0, 0, tiled=True)
    gram = jnp.sum(pieces.astype(F32), axis=0).astype(BF)

    gram_panel = panel_of(gram)
    gram_slab = slab_by_permutes(gram)
    square = product(gram_slab, gram_panel)
    poly = (CUBIC_COEF * gram.astype(F32) + QUINTIC_COEF * square).astype(BF)
    poly_panel = panel_of(poly)
    cubic = LINEAR_COEF * gram.astype(F32) + product(gram_slab, poly_panel)
    once = LINEAR_COEF * iterate + apply(poly_panel, whole)
    cubic_b, once_b = tie(cubic.astype(BF), once.astype(BF))
    ring = Ring(once_b, "row")
    ring.hop()
    gram1 = LINEAR_COEF * cubic + product(slab_of(cubic_b), poly_panel)
    gram1 = ring.tie(gram1.astype(BF))
    ring.hop()
    gram1_panel = panel_of(gram1)
    square1 = product(slab_by_permutes(gram1), gram1_panel)
    poly1 = (CUBIC_COEF * gram1.astype(F32) + QUINTIC_COEF * square1).astype(BF)
    poly1 = ring.tie(poly1)
    ring.hop()
    ring.hop()
    poly1_panel = panel_of(poly1)
    twice = LINEAR_COEF * once + apply(poly1_panel, in_order(ring.blocks, "row"))
    return (math.sqrt(K) * twice).astype(BF)


def solution(mesh):
    in_specs = (P("row", ("col", "ka")),)
    out_specs = P("row", ("col", "ka"))
    return jax.shard_map(body, mesh=mesh, in_specs=in_specs, out_specs=out_specs, check_vma=False)
```

```python
import math

import jax
import jax.numpy as jnp
from jax import lax
from jax.experimental import pallas as pl
from jax.experimental.pallas import tpu as pltpu
from jax.sharding import PartitionSpec as P

K = 13824

LINEAR_COEF = 3.4445
CUBIC_COEF = -4.775
QUINTIC_COEF = 2.0315


BF = jnp.bfloat16
F32 = jnp.float32
VMEM = pl.BlockSpec(memory_space=pltpu.VMEM)
GRANT = 16 << 20
SMEM = pl.BlockSpec(memory_space=pltpu.SMEM)


def shift(array, axis, step):
    n = lax.axis_size(axis)
    return lax.ppermute(array, axis, [((i + step) % n, i) for i in range(n)])


def tie(*arrays):
    return lax.optimization_barrier(arrays)


def put(out, block, place, dim):
    return lax.dynamic_update_slice_in_dim(out, block, place * block.shape[dim], dim)


def in_order(blocks, axis):
    n = lax.axis_size(axis)
    here = lax.axis_index(axis)
    out = jnp.zeros((n * blocks[0].shape[0], *blocks[0].shape[1:]), blocks[0].dtype)
    for step, block in enumerate(blocks):
        out = put(out, block, lax.rem(here + step, n), 0)
    return out


def ring_gather(array, axis):
    n = lax.axis_size(axis)
    here = lax.axis_index(axis)

    def step(s, carry):
        out, up, down = carry
        later = shift(up, axis, 1), shift(down, axis, -1)
        out = put(out, up, lax.rem(here + s, n), 0)
        out = put(out, down, lax.rem(here + n - s, n), 0)
        return (out, *later)

    out = jnp.zeros((n * array.shape[0], *array.shape[1:]), array.dtype)
    out, up, _ = lax.fori_loop(0, n // 2, step, (out, array, array))
    return put(out, up, lax.rem(here + n // 2, n), 0)


class Ring:
    def __init__(self, array, axis):
        self.axis, self.n = axis, lax.axis_size(axis)
        self.blocks = [None] * self.n
        self.blocks[0] = array
        self.step = 0

    def hop(self):
        self.step += 1
        s, n = self.step, self.n
        self.blocks[s] = shift(self.blocks[s - 1], self.axis, 1)
        if n - s > s:
            self.blocks[n - s] = shift(self.blocks[(n - s + 1) % n], self.axis, -1)

    def tie(self, array):
        s, n = self.step, self.n
        at = [s] if n - s <= s else [s, n - s]
        out = tie(*(self.blocks[i] for i in at), array)
        for i, block in zip(at, out):
            self.blocks[i] = block
        return out[-1]


def swap(array):
    return lax.ppermute(array, "ka", [(0, 1), (1, 0)])


def from_everyone(array, axis):
    n = lax.axis_size(axis)
    return lax.all_to_all(jnp.broadcast_to(array[None], (n, *array.shape)), axis, 0, 0, tiled=True)


def gram_kernel(where, whole, own, mine, theirs):
    rows = own.shape[0]
    n = whole.shape[0] // rows
    ka = where[1]
    for j in range(n):
        block = lax.dot_general(
            whole[j * rows : (j + 1) * rows, :],
            own[...],
            (((1,), (1,)), ((), ())),
            preferred_element_type=F32,
        ).astype(BF)
        half, at = divmod(j, n // 2)
        place = slice(at * rows, (at + 1) * rows)

        @pl.when(ka == half)
        def _():
            mine[place, :] = block

        @pl.when(ka != half)
        def _():
            theirs[place, :] = block


def partial_gram(where, whole, own):
    rows = own.shape[0]
    half = jax.ShapeDtypeStruct((whole.shape[0] // 2, rows), BF)
    return pl.pallas_call(
        gram_kernel,
        out_shape=(half, half),
        in_specs=[SMEM, VMEM, VMEM],
        out_specs=(VMEM, VMEM),
        compiler_params=pltpu.CompilerParams(vmem_limit_bytes=GRANT),
        cost_estimate=pl.CostEstimate(
            flops=2 * whole.size * rows, bytes_accessed=2 * whole.size, transcendentals=0
        ),
    )(where, whole, own)


def product(where, blocks, panel, add, scale, times, outs):
    listed = isinstance(blocks, list)
    blocks = blocks if listed else [blocks]
    n = 8
    height, width = add.shape

    def kernel(where_ref, *refs):
        slabs = refs[: len(blocks)]
        mine, theirs, add_ref = refs[len(blocks) : len(blocks) + 3]
        out_refs = refs[len(blocks) + 3 : len(blocks) + 3 + len(outs)]
        z, ka = where_ref[0], where_ref[1]
        if listed:
            slab = refs[-1]
            for s, ref in enumerate(slabs):
                slab[lax.rem(z + s, n)] = ref[...]
        else:
            slab = slabs[0]
        total = jnp.zeros((height, width), F32)
        for side, part in ((ka, mine), (1 - ka, theirs)):
            for at in range(n // 2):
                total += jnp.dot(
                    slab[side * (n // 2) + at],
                    part[at * width : (at + 1) * width, :],
                    preferred_element_type=F32,
                )
        value = scale * add_ref[...].astype(F32) + times * total
        for ref in out_refs:
            ref[...] = value.astype(ref.dtype)

    out = pl.pallas_call(
        kernel,
        out_shape=tuple(jax.ShapeDtypeStruct((height, width), kind) for kind in outs),
        in_specs=[SMEM] + [VMEM] * (len(blocks) + 3),
        out_specs=tuple([VMEM] * len(outs)),
        scratch_shapes=[pltpu.VMEM((n, height, width), BF)] if listed else [],
        compiler_params=pltpu.CompilerParams(vmem_limit_bytes=GRANT),
        cost_estimate=pl.CostEstimate(
            flops=2 * n * height * width * width, bytes_accessed=2 * n * width * width, transcendentals=0
        ),
    )(where, *blocks, *panel, add)
    return out if len(outs) > 1 else out[0]


def both_halves(mine):
    rows = mine.shape[-1]
    return mine.reshape(-1, rows), swap(mine).reshape(-1, rows)


def halves(block):
    return both_halves(from_everyone(block, "col"))


def halves_and_slab(block):
    n = lax.axis_size("row")
    mine = from_everyone(block, "col")
    blocks = [block] + [shift(block, "row", s) for s in range(1, n)]
    mine, *blocks = tie(mine, *blocks)
    return both_halves(mine), blocks


def whole_panel(panel):
    mine, theirs = panel
    first = lax.axis_index("ka") == 0
    return jnp.concatenate([jnp.where(first, mine, theirs), jnp.where(first, theirs, mine)], axis=0)


def apply(panel, whole):
    return lax.dot_general(whole_panel(panel), whole, (((0,), (0,)), ((), ())), preferred_element_type=F32)


def body(iterate):
    rows = iterate.shape[0]
    where = jnp.stack([lax.axis_index("row"), lax.axis_index("ka")]).astype(jnp.int32)
    cols = lax.axis_size("col")
    xb = iterate.astype(BF)
    whole = ring_gather(xb, "row")

    mine, theirs = partial_gram(where, whole, xb)
    mine, theirs = (part.reshape(cols, -1, rows) for part in (mine, theirs))
    summed = (mine.astype(F32) + swap(theirs).astype(F32)).astype(BF)
    pieces = lax.all_to_all(summed, "col", 0, 0, tiled=True)
    gram = jnp.sum(pieces.astype(F32), axis=0).astype(BF)

    gram_panel, gram_slab = halves_and_slab(gram)
    poly = product(where, gram_slab, gram_panel, gram, CUBIC_COEF, QUINTIC_COEF, (BF,))
    poly_panel = halves(poly)
    cubic, cubic_b = product(where, gram_slab, poly_panel, gram, LINEAR_COEF, 1.0, (F32, BF))
    once = LINEAR_COEF * iterate + apply(poly_panel, whole)
    cubic_b, once_b = tie(cubic_b, once.astype(BF))
    ring = Ring(once_b, "row")
    ring.hop()
    gram1 = product(where, from_everyone(cubic_b, "row"), poly_panel, cubic, LINEAR_COEF, 1.0, (BF,))
    gram1 = ring.tie(gram1)
    ring.hop()
    gram1_panel, gram1_slab = halves_and_slab(gram1)
    poly1 = product(where, gram1_slab, gram1_panel, gram1, CUBIC_COEF, QUINTIC_COEF, (BF,))
    poly1 = ring.tie(poly1)
    ring.hop()
    ring.hop()
    poly1_panel = halves(poly1)
    twice = LINEAR_COEF * once + apply(poly1_panel, in_order(ring.blocks, "row"))
    return (math.sqrt(K) * twice).astype(BF)


def solution(mesh):
    in_specs = (P("row", ("col", "ka")),)
    out_specs = P("row", ("col", "ka"))
    return jax.shard_map(body, mesh=mesh, in_specs=in_specs, out_specs=out_specs, check_vma=False)
```
